512 devices in a mesh: expert: 8 (over z_lo, x), fsdp: 64 (over z_hi, y, core).
Axes of the slice: x: 4, y: 8, z: 8 (z_hi: 4, z_lo: 2; z = z_hi * 2 + z_lo), core: 2. Of those that a mesh axis runs over, the one named last changes fastest.
Arguments:
- dense_rows: bfloat16 [128, 14336], P('fsdp', 'expert'), may hold values from -6 to 6
- noise: bfloat16 [8, 128, 14336], P('expert', 'fsdp'), may hold values from -6 to 6
- features: bfloat16 [8, 8192, 128], P('expert', 'fsdp'), may hold values from -16 to 16
- out_grads: bfloat16 [8, 8192, 14336], P('expert', 'fsdp'), may hold values from -1 to 1
Outputs:
- master: float32 [8, 128, 14336], P('expert', 'fsdp')
- first_moment: float32 [8, 128, 14336], P('expert', 'fsdp')
- second_moment: float32 [8, 128, 14336], P('expert', 'fsdp')
- expert_copy: bfloat16 [8, 128, 14336], P('expert')
The draws below stay inside these ranges and needn't reach their ends.
All inputs are finite; a program needn't handle non-finite values.
Results may differ from the reference program's by a relative error of at most 0.004.
Values may be sent and summed in bfloat16 or wider, within the bound.
No kernel may reach another device: no remote copies, remote signals or barrier semaphores. Data moves between devices by JAX's collectives and lax.ppermute only.
A program may use at most 64 MiB of HBM per device.

```python
import jax
import jax.numpy as jnp
from jax import lax

FF = 14336
TOK_DEV = 128
EXPERTS = 8
ROWS = 128
TOKENS = 8192
N_FSDP = 64


def raised(array, own_key, source, target, blocks, factor):
    owner, partner = [(jnp.arange(array.shape[position]) // (array.shape[position] // blocks)).reshape([-1 if axis == position else 1 for axis in range(array.ndim)]) for position in (source, target)]
    chosen = jax.random.permutation(own_key, blocks)[partner]
    strong = (owner == chosen) | (owner == (partner + blocks // 2) % blocks)
    return jnp.where(strong, factor * array, array)


def steps_of(rng, dims, split, low, top_value):
    def one(position, shards_of):
        heights = jax.random.uniform(jax.random.fold_in(jax.random.fold_in(rng, 6), position), (shards_of,), jnp.float32, low / len(split), top_value / len(split))
        return jnp.repeat(jnp.exp(heights), dims[position] // shards_of).reshape((-1,) + (1,) * (len(dims) - position - 1))

    level = one(*split[0])
    for cut in split[1:]:
        level = level * one(*cut)
    return level


def normal_values(own_key, dims, width, limit, cuts=(), dtype=jnp.bfloat16):
    values = width * jax.random.normal(own_key, dims, jnp.float32)
    if cuts:
        values = values * steps_of(own_key, dims, cuts, -0.22, 0.18)
    return jnp.clip(values, -limit, limit).astype(dtype)


def bell_draw_with(key, shape, width, most, cuts, heavy, kind=jnp.bfloat16):
    drawn = width * jax.random.normal(key, shape, jnp.float32)
    if cuts:
        drawn = drawn * steps_of(key, shape, cuts, -0.22, 0.18)
    return jnp.clip(raised(drawn, jax.random.fold_in(key, 3), *heavy), -most, most).astype(kind)


def setup_inputs(seed: int = 0) -> dict:
    splits = jax.random.split(jax.random.key(seed), 5)
    dense_rows = normal_values(splits[0], (ROWS, FF), 1.0, 6.0, ((0, 64), (1, 8)))
    noise = normal_values(splits[1], (EXPERTS, ROWS, FF), 1.0, 6.0, ((0, 8), (1, 64)))
    features = bell_draw_with(splits[2], (EXPERTS, TOKENS, ROWS), 1.0, 16.0, ((0, 8), (1, 64)), (1, 2, 64, 4.0))
    out_grads = normal_values(splits[3], (EXPERTS, TOKENS, FF), 0.125, 1.0, ((0, 8), (1, 64)))
    return dict(dense_rows=dense_rows, noise=noise, features=features, out_grads=out_grads)


noise_scale = 0.1
first_decay = 0.9
second_decay = 0.95
learn_rate = 0.2
weight_decay = 0.5
epsilon_adam = 1.0

def expert_gradient(paired):
    inputs_block, grads_block = paired
    stacked_inputs = inputs_block.reshape(N_FSDP, TOK_DEV, ROWS).astype(jnp.float32)
    stacked_grads = grads_block.reshape(N_FSDP, TOK_DEV, FF).astype(jnp.float32)
    partial_value = jnp.einsum('str,stc->src', stacked_inputs, stacked_grads).astype(jnp.bfloat16)
    partial_value = lax.optimization_barrier(partial_value)
    return lax.optimization_barrier(jnp.sum(partial_value.astype(jnp.float32), axis=0))

def adamw(initial, gradient):
    first_moment = (1.0 - first_decay) * gradient
    second_moment = (1.0 - second_decay) * gradient * gradient
    update = first_moment / (1.0 - first_decay) / (jnp.sqrt(second_moment / (1.0 - second_decay)) + epsilon_adam)
    master = initial - learn_rate * (update + weight_decay * initial)
    return (master, first_moment, second_moment)

def reference(dense_rows, noise, features, out_grads):
    initial = dense_rows.astype(jnp.float32)[None] + noise_scale * noise.astype(jnp.float32)
    gradient = lax.map(expert_gradient, (features, out_grads))
    master, first_moment, second_moment = adamw(initial, gradient)
    return (master, first_moment, second_moment, master.astype(jnp.bfloat16))
```

```python
import jax
import jax.numpy as jnp
from jax import lax
from jax.experimental import pallas as pl
from jax.experimental.pallas import tpu as pltpu
from jax.sharding import PartitionSpec as P

noise_scale = 0.1
first_decay = 0.9
second_decay = 0.95
learn_rate = 0.2
weight_decay = 0.5
epsilon_adam = 1.0

FF = 14336
HALF = FF // 2
ROWS = 128
TOK = 128
NZ, NY = 4, 8
F32 = jnp.float32
BF16 = jnp.bfloat16


def index(z, y, c):
    return (z * NY + y) * 2 + c


def perm(target):
    return [
        (index(z, y, c), index(*target(z, y, c)))
        for z in range(NZ)
        for y in range(NY)
        for c in range(2)
    ]


def send(x, target):
    return lax.ppermute(x, "fsdp", perm(target))


def along_y(z, y, c, k):
    return (z, 2 * ((y // 2) ^ k) + y % 2, c)


def along_z(z, y, c, k):
    return (z ^ k, y, c)


def wide(k):
    return lambda z, y, c: along_y(z, y, c, k) if c == 0 else along_z(z, y, c, k)


def narrow(k):
    return lambda z, y, c: along_z(z, y, c, k) if c == 0 else along_y(z, y, c, k)


def neighbour(z, y, c):
    return (z, y ^ 1, c)


def other_core(z, y, c):
    return (z, y, 1 - c)


def adamw(initial, gradient):
    first_moment = (1.0 - first_decay) * gradient
    second_moment = (1.0 - second_decay) * gradient * gradient
    update = (
        first_moment
        / (1.0 - first_decay)
        / (jnp.sqrt(second_moment / (1.0 - second_decay)) + epsilon_adam)
    )
    master = initial - learn_rate * (update + weight_decay * initial)
    return (master, first_moment, second_moment)


def cost(flops, nbytes):
    return pl.CostEstimate(flops=flops, bytes_accessed=nbytes, transcendentals=0)


def params(mib):
    return pltpu.CompilerParams(vmem_limit_bytes=mib << 20)


def shape(rows, dtype):
    return jax.ShapeDtypeStruct((rows, HALF), dtype)


def product_kernel(place, f_own, f_oth, g_own, g_oth, own, s1, s2, s3, left):
    @pl.when(pl.program_id(0) == 0)
    def _():
        c, o, t = place[0], place[1], place[2]
        slot = lax.broadcasted_iota(jnp.int32, (ROWS, ROWS), 0)
        row = lax.broadcasted_iota(jnp.int32, (ROWS, ROWS), 1)
        a = (slot >> 5) ^ o
        b = ((slot >> 3) & 3) ^ t
        block = jnp.where(c == 0, b * 4 + a, a * 4 + b)
        pick = (block * 8 + (slot & 7) == row).astype(F32).astype(BF16)
        for half, f in ((0, f_own), (1, f_oth)):
            left[half] = lax.dot_general(
                pick, f[...], (((1,), (1,)), ((), ())), preferred_element_type=F32
            ).astype(BF16)

    total = jnp.dot(left[0], g_own[...], preferred_element_type=F32).astype(BF16).astype(F32)
    total += jnp.dot(left[1], g_oth[...], preferred_element_type=F32).astype(BF16).astype(F32)
    own[...] = total[:32]
    for k, s in ((1, s1), (2, s2), (3, s3)):
        s[...] = total[32 * k : 32 * k + 32].astype(BF16)


def product(place, f_own, f_oth, grads, g_oth):
    n = 1792
    steps = HALF // n
    small = pl.BlockSpec((TOK, ROWS), lambda i, place: (0, 0))
    part = pl.BlockSpec((32, n), lambda i, place: (0, i))
    return pl.pallas_call(
        product_kernel,
        grid_spec=pltpu.PrefetchScalarGridSpec(
            num_scalar_prefetch=1,
            grid=(steps,),
            in_specs=[
                small,
                small,
                pl.BlockSpec((TOK, n), lambda i, place: (0, place[0] * steps + i)),
                pl.BlockSpec((TOK, n), lambda i, place: (0, i)),
            ],
            out_specs=[part] * 4,
            scratch_shapes=[pltpu.VMEM((2, ROWS, TOK), BF16)],
        ),
        out_shape=[shape(32, F32)] + [shape(32, BF16)] * 3,
        cost_estimate=cost(4 * ROWS * TOK * HALF, 6 * TOK * HALF),
        compiler_params=params(12),
    )(place, f_own, f_oth, grads, g_oth)


def first_sum_kernel(own, r1, r2, r3, keep, t1, t2, t3):
    total = own[...] + (r1[...].astype(F32) + r2[...].astype(F32) + r3[...].astype(F32))
    keep[...] = total[:8]
    for j, t in ((1, t1), (2, t2), (3, t3)):
        t[...] = total[8 * j : 8 * j + 8].astype(BF16)


def first_sum(own, parts):
    n = 1792
    part = pl.BlockSpec((32, n), lambda i: (0, i))
    out = pl.BlockSpec((8, n), lambda i: (0, i))
    return pl.pallas_call(
        first_sum_kernel,
        grid=(HALF // n,),
        in_specs=[part] * 4,
        out_specs=[out] * 4,
        out_shape=[shape(8, F32)] + [shape(8, BF16)] * 3,
        cost_estimate=cost(4 * 32 * HALF, 12 * 32 * HALF),
        compiler_params=params(12),
    )(own, *parts)


def second_sum_kernel(own, r1, r2, r3, out):
    total = own[...] + (r1[...].astype(F32) + r2[...].astype(F32) + r3[...].astype(F32))
    out[...] = total.astype(BF16)


def second_sum(own, parts):
    return pl.pallas_call(
        second_sum_kernel,
        out_shape=shape(8, BF16),
        cost_estimate=cost(4 * 8 * HALF, 12 * 8 * HALF),
        compiler_params=params(12),
    )(own, *parts)


def update_kernel(place, mine, theirs, dense, noise, copy, keep, give):
    c, p = place[0], place[3]
    gradient = mine[...].astype(F32) + theirs[...].astype(F32)
    initial = dense[...].astype(F32) + noise_scale * noise[...].astype(F32)
    copy[...] = adamw(initial, gradient)[0].astype(BF16)

    def rows_of(core):
        lower = jnp.where(core == 0, gradient[0:2], gradient[2:4])
        upper = jnp.where(core == 0, gradient[4:6], gradient[6:8])
        return jnp.where(p == 0, lower, upper)

    keep[...] = rows_of(c)
    give[...] = rows_of(1 - c)


def update(place, mine, theirs, dense, noise):
    return pl.pallas_call(
        update_kernel,
        in_specs=[pl.BlockSpec(memory_space=pltpu.SMEM)]
        + [pl.BlockSpec(memory_space=pltpu.VMEM)] * 4,
        out_shape=[shape(8, BF16), shape(2, F32), shape(2, F32)],
        cost_estimate=cost(20 * 8 * HALF, 12 * 8 * HALF),
        compiler_params=params(12),
    )(place, mine, theirs, dense, noise)


def assemble_kernel(place, *refs):
    blocks, out, sem = refs[:8], refs[8], refs[9]
    c, o, t = place[0], place[1], place[2]
    copies = []
    for half in range(2):
        for k in range(4):
            for j in range(4):
                if half == 0:
                    a, b, core = o ^ k, t ^ j, c
                else:
                    a, b, core = t ^ k, o ^ j, 1 - c
                block = jnp.where(core == 0, b * 4 + a, a * 4 + b)
                copies.append(
                    pltpu.make_async_copy(
                        blocks[half * 4 + k].at[pl.ds(8 * j, 8)],
                        out.at[
                            pl.ds(pl.multiple_of(block * 8, 8), 8),
                            pl.ds(pl.multiple_of(core * HALF, 128), HALF),
                        ],
                        sem.at[len(copies)],
                    )
                )
    for copy in copies:
        copy.start()
    for copy in copies:
        copy.wait()


def assemble(place, blocks):
    return pl.pallas_call(
        assemble_kernel,
        in_specs=[pl.BlockSpec(memory_space=pltpu.SMEM)]
        + [pl.BlockSpec(memory_space=pl.ANY)] * 8,
        out_specs=pl.BlockSpec(memory_space=pl.ANY),
        out_shape=jax.ShapeDtypeStruct((ROWS, FF), BF16),
        scratch_shapes=[pltpu.SemaphoreType.DMA((32,))],
        cost_estimate=cost(0, 4 * ROWS * FF),
        compiler_params=params(12),
    )(place, *blocks)


def in_order(bit, mine, theirs, axis):
    lower = jnp.where(bit == 0, mine, theirs)
    upper = jnp.where(bit == 0, theirs, mine)
    return jnp.concatenate([lower, upper], axis)


def body(dense_rows, noise, features, out_grads):
    f, e = lax.axis_index("fsdp"), lax.axis_index("expert")
    c, y, z = f % 2, (f // 2) % NY, f // (2 * NY)
    q, p = y // 2, y % 2
    o, t = jnp.where(c == 0, q, z), jnp.where(c == 0, z, q)
    place = jnp.stack([c, o, t, p]).astype(jnp.int32)

    grads = out_grads[0]
    f_in = send(features[0], other_core)
    g_in = send(lax.dynamic_slice(grads, (0, (1 - c) * HALF), (TOK, HALF)), other_core)

    dense = dense_rows
    for bit in (1, 2, 4):
        theirs = lax.ppermute(dense, "expert", [(i, i ^ bit) for i in range(8)])
        dense = in_order(e & bit, dense, theirs, 1)
    both = jnp.stack([dense, noise[0]])
    near = lax.dynamic_slice(both, (0, 0, c * HALF), (2, 2, HALF))
    far = lax.dynamic_slice(both, (0, 0, (1 - c) * HALF), (2, 2, HALF))
    wider = in_order(c, near, send(far, other_core), 1)
    wider = in_order(p, wider, send(wider, neighbour), 1)

    own, *chunks = product(place, features[0], f_in, grads, g_in)
    got = [send(x, wide(k)) for k, x in zip((3, 2, 1), chunks[::-1])]
    own, *chunks = first_sum(own, got)
    got = [send(x, narrow(k)) for k, x in zip((3, 2, 1), chunks[::-1])]
    mine = second_sum(own, got)
    theirs = send(mine, neighbour)
    copy, keep, give = update(place, mine, theirs, wider[0], wider[1])

    gathered = [copy] + [send(copy, narrow(k)) for k in (1, 2, 3)]
    gathered = jnp.concatenate(gathered, 0)
    blocks = [gathered] + [send(gathered, wide(k)) for k in (1, 2, 3)]
    blocks += [send(x, other_core) for x in blocks]
    expert_copy = assemble(place, blocks)

    gradient = in_order(c, keep, send(give, other_core), 1)
    initial = dense.astype(F32) + noise_scale * noise[0].astype(F32)
    master, first_moment, second_moment = adamw(initial, gradient)
    return (master[None], first_moment[None], second_moment[None], expert_copy[None])


def solution(mesh):
    return jax.shard_map(
        body,
        mesh=mesh,
        in_specs=(
            P("fsdp", "expert"),
            P("expert", "fsdp", None),
            P("expert", "fsdp", None),
            P("expert", "fsdp", None),
        ),
        out_specs=(
            P("expert", "fsdp", None),
            P("expert", "fsdp", None),
            P("expert", "fsdp", None),
            P("expert", None, None),
        ),
        check_vma=False,
    )
```

```python
import functools

import jax
import jax.numpy as jnp
from jax import lax
from jax.experimental import pallas as pl
from jax.experimental.pallas import tpu as pltpu
from jax.sharding import PartitionSpec as P

noise_scale = 0.1
first_decay = 0.9
second_decay = 0.95
learn_rate = 0.2
weight_decay = 0.5
epsilon_adam = 1.0

FF = 14336
HALF = FF // 2
ROWS = 128
TOK = 128
NZ, NY = 4, 8
F32 = jnp.float32
BF16 = jnp.bfloat16


def index(z, y, c):
    return (z * NY + y) * 2 + c


def perm(target):
    return [
        (index(z, y, c), index(*target(z, y, c)))
        for z in range(NZ)
        for y in range(NY)
        for c in range(2)
    ]


def send(x, target):
    return lax.ppermute(x, "fsdp", perm(target))


def along_y(z, y, c, k):
    return (z, 2 * ((y // 2) ^ k) + y % 2, c)


def along_z(z, y, c, k):
    return (z ^ k, y, c)


def wide(k):
    return lambda z, y, c: along_y(z, y, c, k) if c == 0 else along_z(z, y, c, k)


MIDDLE = [[index(z, 2 * q + p, 0) for z in range(NZ) for p in range(2)] for q in range(4)] + [
    [index(z, y, 1) for y in range(NY)] for z in range(NZ)
]


def swap(x):
    return lax.all_to_all(x, "fsdp", 0, 0, axis_index_groups=MIDDLE, tiled=True)


def other_core(z, y, c):
    return (z, y, 1 - c)


def adamw(initial, gradient):
    first_moment = (1.0 - first_decay) * gradient
    second_moment = (1.0 - second_decay) * gradient * gradient
    update = (
        first_moment
        / (1.0 - first_decay)
        / (jnp.sqrt(second_moment / (1.0 - second_decay)) + epsilon_adam)
    )
    master = initial - learn_rate * (update + weight_decay * initial)
    return (master, first_moment, second_moment)


def cost(flops, nbytes):
    return pl.CostEstimate(flops=flops, bytes_accessed=nbytes, transcendentals=0)


def params(mib):
    return pltpu.CompilerParams(vmem_limit_bytes=mib << 20)


def shape(rows, dtype):
    return jax.ShapeDtypeStruct((rows, HALF), dtype)


VMEM = pl.BlockSpec(memory_space=pltpu.VMEM)
HBM = pl.BlockSpec(memory_space=pltpu.HBM)
SMEM = pl.BlockSpec(memory_space=pltpu.SMEM)
TILE = 896
FOLD = HALF // 2
FIRST = 60
FAR_FIRST = (2, 1, 3)


def in_slots(c, o, features):
    slot = lax.broadcasted_iota(jnp.int32, (ROWS, ROWS), 0)
    row = lax.broadcasted_iota(jnp.int32, (ROWS, ROWS), 1)
    a = (slot >> 5) ^ o
    b = (slot >> 3) & 3
    block = jnp.where(c == 0, b * 4 + a, a * 4 + b)
    pick = (block * 8 + (slot & 7) == row).astype(F32).astype(BF16)
    return lax.dot_general(
        pick, features, (((1,), (1,)), ((), ())), preferred_element_type=F32
    ).astype(BF16)


def product_kernel(far, place, features, grads, out, part, sem):
    c, o, t = place[0], place[1], place[2]
    core, first = (1 - c, t) if far else (c, o)
    copies = [
        pltpu.make_async_copy(
            grads.at[:, pl.ds(pl.multiple_of(core * HALF + n, 128), TILE)],
            part.at[:, pl.ds(n, TILE)],
            sem.at[n // TILE],
        )
        for n in range(0, HALF, TILE)
    ]
    for copy in copies:
        copy.start()
    left = in_slots(core, first, features[...])
    for i, copy in enumerate(copies):
        copy.wait()
        n = slice(i * TILE, (i + 1) * TILE)
        out[:, n] = jnp.dot(left, part[:, n], preferred_element_type=F32).astype(BF16)


def product(far, place, features, grads):
    return pl.pallas_call(
        functools.partial(product_kernel, far),
        in_specs=[SMEM, VMEM, HBM],
        out_specs=VMEM,
        out_shape=shape(ROWS, BF16),
        scratch_shapes=[pltpu.VMEM((TOK, HALF), BF16), pltpu.SemaphoreType.DMA((HALF // TILE,))],
        cost_estimate=cost(2 * ROWS * TOK * HALF, 4 * TOK * HALF),
        compiler_params=params(FIRST if far else 12),
    )(place, features, grads)


def chip_sum_kernel(near, far, own, s1, s2, s3):
    for k, s in ((0, own), (1, s1), (2, s2), (3, s3)):
        n = slice(32 * k, 32 * k + 32)
        s[...] = (near[n, :].astype(F32) + far[n, :].astype(F32)).astype(s.dtype)


def chip_sum(near, far):
    return pl.pallas_call(
        chip_sum_kernel,
        in_specs=[VMEM] * 2,
        out_specs=[VMEM] * 4,
        out_shape=[shape(32, F32)] + [shape(32, BF16)] * 3,
        cost_estimate=cost(ROWS * HALF, 6 * ROWS * HALF),
        compiler_params=params(12),
    )(near, far)


def first_sum_kernel(own, r1, r2, r3, total, out):
    for m in range(0, 32, 4):
        parts = []
        for h in range(2):
            n = (slice(m, m + 4), slice(h * FOLD, (h + 1) * FOLD))
            rest = r1[n].astype(F32) + r2[n].astype(F32) + r3[n].astype(F32)
            parts.append(own[n] + rest)
        value = jnp.concatenate(parts, 0)
        total[2 * m : 2 * m + 8, :] = value
        out[2 * m : 2 * m + 8, :] = value.astype(BF16)


def first_sum(own, parts):
    return pl.pallas_call(
        first_sum_kernel,
        in_specs=[VMEM] * 4,
        out_specs=[VMEM] * 2,
        out_shape=[jax.ShapeDtypeStruct((64, FOLD), d) for d in (F32, BF16)],
        cost_estimate=cost(4 * 32 * HALF, 12 * 32 * HALF),
        compiler_params=params(12),
    )(own, *parts)


def update_kernel(place, total, parts, mine, theirs, copy, keep, give):
    c = place[0]
    own = place[2] * 2 + place[3]
    gradient = total[pl.ds(pl.multiple_of(8 * own, 8), 8), :]
    for m in range(8):
        part = parts[8 * m : 8 * m + 8, :].astype(F32)
        gradient += jnp.where(own == m, 0.0, part)

    def folded(i):
        near, far = mine[i].astype(F32), theirs[i].astype(F32)
        low, high = jnp.where(c == 0, near, far), jnp.where(c == 0, far, near)
        rows = [x[:, h * FOLD : (h + 1) * FOLD] for h in range(2) for x in (low, high)]
        return jnp.concatenate(rows, 0)

    initial = folded(0) + noise_scale * folded(1)
    master = adamw(initial, gradient)[0].astype(BF16)
    for m in range(8):
        copy[8 * m : 8 * m + 8, :] = master
    for h in range(2):
        low, high = gradient[4 * h : 4 * h + 2], gradient[4 * h + 2 : 4 * h + 4]
        n = slice(h * FOLD, (h + 1) * FOLD)
        keep[:, n] = jnp.where(c == 0, low, high)
        give[:, n] = jnp.where(c == 0, high, low)


def update(place, total, parts, mine, theirs):
    return pl.pallas_call(
        update_kernel,
        in_specs=[SMEM] + [VMEM] * 4,
        out_specs=[VMEM] * 3,
        out_shape=[jax.ShapeDtypeStruct((64, FOLD), BF16), shape(2, F32), shape(2, F32)],
        cost_estimate=cost(20 * 8 * FOLD, 40 * 8 * FOLD),
        compiler_params=params(12),
    )(place, total, parts, mine, theirs)


def unfold_kernel(folded, out):
    for t in range(4):
        for h in range(2):
            n = 16 * t + 4 * h
            value = [folded[n + 8 * p : n + 8 * p + 4, :].astype(F32) for p in range(2)]
            out[8 * t : 8 * t + 8, h * FOLD : (h + 1) * FOLD] = jnp.concatenate(value, 0).astype(BF16)


def unfold(folded):
    return pl.pallas_call(
        unfold_kernel,
        in_specs=[VMEM],
        out_specs=VMEM,
        out_shape=shape(32, BF16),
        cost_estimate=cost(0, 4 * 32 * HALF),
        compiler_params=params(12),
    )(folded)


def assemble_kernel(place, *refs):
    blocks, out, sem = refs[:8], refs[8], refs[9]
    c, o, t = place[0], place[1], place[2]
    copies = []
    for half in range(2):
        for k in range(4):
            for j in range(4):
                if half == 0:
                    a, b, core = o ^ ((0,) + FAR_FIRST)[k], j, c
                else:
                    a, b, core = t ^ ((0,) + FAR_FIRST)[k], j, 1 - c
                block = jnp.where(core == 0, b * 4 + a, a * 4 + b)
                copies.append(
                    pltpu.make_async_copy(
                        blocks[half * 4 + k].at[pl.ds(8 * j, 8)],
                        out.at[
                            pl.ds(pl.multiple_of(block * 8, 8), 8),
                            pl.ds(pl.multiple_of(core * HALF, 128), HALF),
                        ],
                        sem.at[len(copies)],
                    )
                )
    for copy in copies:
        copy.start()
    for copy in copies:
        copy.wait()


def assemble(place, blocks):
    return pl.pallas_call(
        assemble_kernel,
        in_specs=[SMEM] + [pl.BlockSpec(memory_space=pl.ANY)] * 8,
        out_specs=HBM,
        out_shape=jax.ShapeDtypeStruct((ROWS, FF), BF16),
        scratch_shapes=[pltpu.SemaphoreType.DMA((32,))],
        cost_estimate=cost(0, 4 * ROWS * FF),
        compiler_params=params(12),
    )(place, *blocks)


def in_order(bit, mine, theirs, axis):
    lower = jnp.where(bit == 0, mine, theirs)
    upper = jnp.where(bit == 0, theirs, mine)
    return jnp.concatenate([lower, upper], axis)


def body(dense_rows, noise, features, out_grads):
    f, e = lax.axis_index("fsdp"), lax.axis_index("expert")
    c, y, z = f % 2, (f // 2) % NY, f // (2 * NY)
    q, p = y // 2, y % 2
    o, t = jnp.where(c == 0, q, z), jnp.where(c == 0, z, q)
    place = jnp.stack([c, o, t, p]).astype(jnp.int32)

    grads = out_grads[0]
    far = send(product(True, place, features[0], grads), other_core)
    near = product(False, place, features[0], grads)
    own, *chunks = chip_sum(near, far)
    got = [send(chunks[k - 1], wide(k)) for k in FAR_FIRST]
    total, rounded = first_sum(own, got)

    dense = lax.all_to_all(jnp.stack([dense_rows] * 8), "expert", 0, 0, tiled=True)
    dense = dense.swapaxes(0, 1).reshape(2, FF)
    both = jnp.stack([dense, noise[0]])
    mine = lax.dynamic_slice(both, (0, 0, c * HALF), (2, 2, HALF))
    theirs = send(lax.dynamic_slice(both, (0, 0, (1 - c) * HALF), (2, 2, HALF)), other_core)

    copy, keep, give = update(place, total, swap(rounded), mine, theirs)
    gathered = unfold(swap(copy))
    blocks = [gathered] + [send(gathered, wide(k)) for k in FAR_FIRST]
    blocks += [send(x, other_core) for x in blocks]
    expert_copy = assemble(place, blocks)

    gradient = in_order(c, keep, send(give, other_core), 1)
    initial = dense.astype(F32) + noise_scale * noise[0].astype(F32)
    master, first_moment, second_moment = adamw(initial, gradient)
    return (master[None], first_moment[None], second_moment[None], expert_copy[None])


def solution(mesh):
    return jax.shard_map(
        body,
        mesh=mesh,
        in_specs=(
            P("fsdp", "expert"),
            P("expert", "fsdp", None),
            P("expert", "fsdp", None),
            P("expert", "fsdp", None),
        ),
        out_specs=(
            P("expert", "fsdp", None),
            P("expert", "fsdp", None),
            P("expert", "fsdp", None),
            P("expert", None, None),
        ),
        check_vma=False,
    )
```

```python
import functools

import jax
import jax.numpy as jnp
from jax import lax
from jax.experimental import pallas as pl
from jax.experimental.pallas import tpu as pltpu
from jax.sharding import PartitionSpec as P

noise_scale = 0.1
first_decay = 0.9
second_decay = 0.95
learn_rate = 0.2
weight_decay = 0.5
epsilon_adam = 1.0

FF = 14336
HALF = FF // 2
ROWS = 128
TOK = 128
NZ, NY = 4, 8
F32 = jnp.float32
BF16 = jnp.bfloat16


def index(z, y, c):
    return (z * NY + y) * 2 + c


def perm(target):
    return [
        (index(z, y, c), index(*target(z, y, c)))
        for z in range(NZ)
        for y in range(NY)
        for c in range(2)
    ]


def send(x, target):
    return lax.ppermute(x, "fsdp", perm(target))


def along_y(z, y, c, k):
    return (z, 2 * ((y // 2) ^ k) + y % 2, c)


def along_z(z, y, c, k):
    return (z ^ k, y, c)


def wide(k):
    return lambda z, y, c: along_y(z, y, c, k) if c == 0 else along_z(z, y, c, k)


MIDDLE = [[index(z, 2 * q + p, 0) for z in range(NZ) for p in range(2)] for q in range(4)] + [
    [index(z, y, 1) for y in range(NY)] for z in range(NZ)
]


def swap(x):
    return lax.all_to_all(x, "fsdp", 0, 0, axis_index_groups=MIDDLE, tiled=True)


def other_core(z, y, c):
    return (z, y, 1 - c)


def adamw(initial, gradient):
    first_moment = (1.0 - first_decay) * gradient
    second_moment = (1.0 - second_decay) * gradient * gradient
    update = (
        first_moment
        / (1.0 - first_decay)
        / (jnp.sqrt(second_moment / (1.0 - second_decay)) + epsilon_adam)
    )
    master = initial - learn_rate * (update + weight_decay * initial)
    return (master, first_moment, second_moment)


def place():
    f = lax.axis_index("fsdp")
    c, q, z = f & 1, (f >> 2) & 3, f >> 4
    return c, jnp.where(c == 0, q, z), jnp.where(c == 0, z, q)


def cost(flops, nbytes):
    return pl.CostEstimate(flops=flops, bytes_accessed=nbytes, transcendentals=0)


def params(mib):
    return pltpu.CompilerParams(vmem_limit_bytes=mib << 20)


def shape(rows, dtype):
    return jax.ShapeDtypeStruct((rows, HALF), dtype)


VMEM = pl.BlockSpec(memory_space=pltpu.VMEM)
HBM = pl.BlockSpec(memory_space=pltpu.HBM)
TILE = 896
FOLD = HALF // 2


def in_slots(c, o, features):
    slot = lax.broadcasted_iota(jnp.int32, (ROWS, ROWS), 0)
    row = lax.broadcasted_iota(jnp.int32, (ROWS, ROWS), 1)
    a = (slot >> 5) ^ o
    b = (slot >> 3) & 3
    block = jnp.where(c == 0, b * 4 + a, a * 4 + b)
    pick = (block * 8 + (slot & 7) == row).astype(F32).astype(BF16)
    return lax.dot_general(
        pick, features, (((1,), (1,)), ((), ())), preferred_element_type=F32
    ).astype(BF16)


def tiles(source, column, target, sem):
    return [
        pltpu.make_async_copy(
            source.at[:, pl.ds(pl.multiple_of(column + n, 128), TILE)],
            target.at[:, pl.ds(n, TILE)],
            sem.at[n // TILE],
        )
        for n in range(0, HALF, TILE)
    ]


def far_product_kernel(features, grads, out, local, part, value, sem, out_sem):
    c, _, t = place()
    core = 1 - c
    first = pltpu.make_async_copy(features, local, sem.at[HALF // TILE])
    first.start()
    copies = tiles(grads, core * HALF, part, sem)
    for copy in copies:
        copy.start()
    first.wait()
    left = in_slots(core, t, local[...])
    results = tiles(value, 0, out, out_sem)
    for i, (copy, result) in enumerate(zip(copies, results)):
        copy.wait()
        n = slice(i * TILE, (i + 1) * TILE)
        value[:, n] = jnp.dot(left, part[:, n], preferred_element_type=F32).astype(BF16)
        result.start()
    for result in results:
        result.wait()


def far_product(features, grads):
    count = HALF // TILE
    return pl.pallas_call(
        far_product_kernel,
        in_specs=[HBM, HBM],
        out_specs=HBM,
        out_shape=shape(ROWS, BF16),
        scratch_shapes=[
            pltpu.VMEM((TOK, ROWS), BF16),
            pltpu.VMEM((TOK, HALF), BF16),
            pltpu.VMEM((ROWS, HALF), BF16),
            pltpu.SemaphoreType.DMA((count + 1,)),
            pltpu.SemaphoreType.DMA((count,)),
        ],
        cost_estimate=cost(2 * ROWS * TOK * HALF, 4 * TOK * HALF),
        compiler_params=params(60),
    )(features, grads)


def near_product_kernel(features, grads, out, part, sem):
    c, o, _ = place()
    copies = tiles(grads, c * HALF, part, sem)
    for copy in copies:
        copy.start()
    left = in_slots(c, o, features[...])
    for i, copy in enumerate(copies):
        copy.wait()
        n = slice(i * TILE, (i + 1) * TILE)
        out[:, n] = jnp.dot(left, part[:, n], preferred_element_type=F32).astype(BF16)


def near_product(features, grads):
    return pl.pallas_call(
        near_product_kernel,
        in_specs=[VMEM, HBM],
        out_specs=VMEM,
        out_shape=shape(ROWS, BF16),
        scratch_shapes=[pltpu.VMEM((TOK, HALF), BF16), pltpu.SemaphoreType.DMA((HALF // TILE,))],
        cost_estimate=cost(2 * ROWS * TOK * HALF, 4 * TOK * HALF),
        compiler_params=params(12),
    )(features, grads)


def chip_sum_kernel(near, far, own, s1, s2, s3):
    for k, s in ((0, own), (1, s1), (2, s2), (3, s3)):
        n = slice(32 * k, 32 * k + 32)
        s[...] = (near[n, :].astype(F32) + far[n, :].astype(F32)).astype(s.dtype)


def chip_sum(near, far):
    return pl.pallas_call(
        chip_sum_kernel,
        in_specs=[VMEM] * 2,
        out_specs=[VMEM] * 4,
        out_shape=[shape(32, F32)] + [shape(32, BF16)] * 3,
        cost_estimate=cost(ROWS * HALF, 6 * ROWS * HALF),
        compiler_params=params(12),
    )(near, far)


def first_sum_kernel(own, r1, r2, r3, total, out):
    for m in range(0, 32, 4):
        parts = []
        for h in range(2):
            n = (slice(m, m + 4), slice(h * FOLD, (h + 1) * FOLD))
            rest = r1[n].astype(F32) + r2[n].astype(F32) + r3[n].astype(F32)
            parts.append(own[n] + rest)
        value = jnp.concatenate(parts, 0)
        total[2 * m : 2 * m + 8, :] = value
        out[2 * m : 2 * m + 8, :] = value.astype(BF16)


def first_sum(own, parts):
    return pl.pallas_call(
        first_sum_kernel,
        in_specs=[VMEM] * 4,
        out_specs=[VMEM] * 2,
        out_shape=[jax.ShapeDtypeStruct((64, FOLD), d) for d in (F32, BF16)],
        cost_estimate=cost(4 * 32 * HALF, 12 * 32 * HALF),
        compiler_params=params(12),
    )(own, *parts)


def update_kernel(total, parts, mine, theirs, copy, keep, give):
    c, _, t = place()
    own = t * 2 + ((lax.axis_index("fsdp") >> 1) & 1)
    gradient = total[pl.ds(pl.multiple_of(8 * own, 8), 8), :]
    for m in range(8):
        part = parts[8 * m : 8 * m + 8, :].astype(F32)
        gradient += jnp.where(own == m, 0.0, part)

    def folded(i):
        near, far = mine[i].astype(F32), theirs[i].astype(F32)
        low, high = jnp.where(c == 0, near, far), jnp.where(c == 0, far, near)
        rows = [x[:, h * FOLD : (h + 1) * FOLD] for h in range(2) for x in (low, high)]
        return jnp.concatenate(rows, 0)

    initial = folded(0) + noise_scale * folded(1)
    master = adamw(initial, gradient)[0].astype(BF16)
    for m in range(8):
        copy[8 * m : 8 * m + 8, :] = master
    for h in range(2):
        low, high = gradient[4 * h : 4 * h + 2], gradient[4 * h + 2 : 4 * h + 4]
        n = slice(h * FOLD, (h + 1) * FOLD)
        keep[:, n] = jnp.where(c == 0, low, high)
        give[:, n] = jnp.where(c == 0, high, low)


def update(total, parts, mine, theirs):
    return pl.pallas_call(
        update_kernel,
        in_specs=[VMEM] * 4,
        out_specs=[VMEM] * 3,
        out_shape=[jax.ShapeDtypeStruct((64, FOLD), BF16), shape(2, F32), shape(2, F32)],
        cost_estimate=cost(20 * 8 * FOLD, 40 * 8 * FOLD),
        compiler_params=params(12),
    )(total, parts, mine, theirs)


def unfold_kernel(folded, out):
    for t in range(4):
        for h in range(2):
            n = 16 * t + 4 * h
            value = [folded[n + 8 * p : n + 8 * p + 4, :].astype(F32) for p in range(2)]
            out[8 * t : 8 * t + 8, h * FOLD : (h + 1) * FOLD] = jnp.concatenate(value, 0).astype(BF16)


def unfold(folded):
    return pl.pallas_call(
        unfold_kernel,
        in_specs=[VMEM],
        out_specs=VMEM,
        out_shape=shape(32, BF16),
        cost_estimate=cost(0, 4 * 32 * HALF),
        compiler_params=params(12),
    )(folded)


def assemble_kernel(pieces, *refs):
    c, o, t = place()
    blocks, out, sem = refs[: len(pieces)], refs[-2], refs[-1]
    copies = []
    for block, (half, k) in zip(blocks, pieces):
        core, a = (c, o ^ k) if half == 0 else (1 - c, t ^ k)
        for j in range(4):
            row = jnp.where(core == 0, j * 4 + a, a * 4 + j) * 8
            copies.append(
                pltpu.make_async_copy(
                    block.at[pl.ds(8 * j, 8)],
                    out.at[
                        pl.ds(pl.multiple_of(row, 8), 8),
                        pl.ds(pl.multiple_of(core * HALF, 128), HALF),
                    ],
                    sem.at[len(copies)],
                )
            )
    for copy in copies:
        copy.start()
    for copy in copies:
        copy.wait()


def assemble(pieces, blocks, result=None):
    operands = list(blocks) if result is None else list(blocks) + [result]
    return pl.pallas_call(
        functools.partial(assemble_kernel, pieces),
        in_specs=[pl.BlockSpec(memory_space=pl.ANY)] * len(blocks)
        + [HBM] * (len(operands) - len(blocks)),
        out_specs=HBM,
        out_shape=jax.ShapeDtypeStruct((ROWS, FF), BF16),
        scratch_shapes=[pltpu.SemaphoreType.DMA((4 * len(pieces),))],
        input_output_aliases={} if result is None else {len(blocks): 0},
        cost_estimate=cost(0, len(pieces) * ROWS * HALF),
        compiler_params=params(12),
    )(*operands)


def in_order(bit, mine, theirs, axis):
    lower = jnp.where(bit == 0, mine, theirs)
    upper = jnp.where(bit == 0, theirs, mine)
    return jnp.concatenate([lower, upper], axis)


def body(dense_rows, noise, features, out_grads):
    c = lax.axis_index("fsdp") & 1

    grads = out_grads[0]
    far = send(far_product(features[0], grads), other_core)
    near = near_product(features[0], grads)
    own, *chunks = chip_sum(near, far)
    got = [send(chunks[k - 1], wide(k)) for k in (2, 1, 3)]
    total, rounded = first_sum(own, got)

    dense = lax.all_to_all(jnp.stack([dense_rows] * 8), "expert", 0, 0, tiled=True)
    dense = dense.swapaxes(0, 1).reshape(2, FF)
    both = jnp.stack([dense, noise[0]])
    mine = lax.dynamic_slice(both, (0, 0, c * HALF), (2, 2, HALF))
    theirs = send(lax.dynamic_slice(both, (0, 0, (1 - c) * HALF), (2, 2, HALF)), other_core)

    copy, keep, give = update(total, swap(rounded), mine, theirs)
    own = unfold(swap(copy))
    r1, r3, r2 = (send(own, wide(k)) for k in (1, 3, 2))
    x0, x1, x3, x2 = (send(x, other_core) for x in (own, r1, r3, r2))
    early = assemble(((0, 0), (0, 1), (1, 0), (1, 1)), (own, r1, x0, x1))
    expert_copy = assemble(((0, 2), (0, 3), (1, 2), (1, 3)), (r2, r3, x2, x3), early)
    give, _ = lax.optimization_barrier((give, r1))

    gradient = in_order(c, keep, send(give, other_core), 1)
    initial = dense.astype(F32) + noise_scale * noise[0].astype(F32)
    master, first_moment, second_moment = adamw(initial, gradient)
    return (master[None], first_moment[None], second_moment[None], expert_copy[None])


def solution(mesh):
    return jax.shard_map(
        body,
        mesh=mesh,
        in_specs=(
            P("fsdp", "expert"),
            P("expert", "fsdp", None),
            P("expert", "fsdp", None),
            P("expert", "fsdp", None),
        ),
        out_specs=(
            P("expert", "fsdp", None),
            P("expert", "fsdp", None),
            P("expert", "fsdp", None),
            P("expert", None, None),
        ),
        check_vma=False,
    )
```

```python
import functools

import jax
import jax.numpy as jnp
from jax import lax
from jax.experimental import pallas as pl
from jax.experimental.pallas import tpu as pltpu
from jax.sharding import PartitionSpec as P

noise_scale = 0.1
first_decay = 0.9
second_decay = 0.95
learn_rate = 0.2
weight_decay = 0.5
epsilon_adam = 1.0

FF = 14336
HALF = FF // 2
ROWS = 128
TOK = 128
NZ, NY = 4, 8
F32 = jnp.float32
BF16 = jnp.bfloat16


def index(z, y, c):
    return (z * NY + y) * 2 + c


def perm(target):
    return [
        (index(z, y, c), index(*target(z, y, c)))
        for z in range(NZ)
        for y in range(NY)
        for c in range(2)
    ]


def send(x, target):
    return lax.ppermute(x, "fsdp", perm(target))


def along_y(z, y, c, k):
    return (z, 2 * ((y // 2) ^ k) + y % 2, c)


def along_z(z, y, c, k):
    return (z ^ k, y, c)


def wide(k):
    return lambda z, y, c: along_y(z, y, c, k) if c == 0 else along_z(z, y, c, k)


MIDDLE = [[index(z, 2 * q + p, 0) for z in range(NZ) for p in range(2)] for q in range(4)] + [
    [index(z, y, 1) for y in range(NY)] for z in range(NZ)
]


def swap(x):
    return lax.all_to_all(x, "fsdp", 0, 0, axis_index_groups=MIDDLE, tiled=True)


def other_core(z, y, c):
    return (z, y, 1 - c)


def adamw(initial, gradient):
    first_moment = (1.0 - first_decay) * gradient
    second_moment = (1.0 - second_decay) * gradient * gradient
    update = (
        first_moment
        / (1.0 - first_decay)
        / (jnp.sqrt(second_moment / (1.0 - second_decay)) + epsilon_adam)
    )
    master = initial - learn_rate * (update + weight_decay * initial)
    return (master, first_moment, second_moment)


def place():
    f = lax.axis_index("fsdp")
    c, q, z = f & 1, (f >> 2) & 3, f >> 4
    return c, jnp.where(c == 0, q, z), jnp.where(c == 0, z, q)


def cost(flops, nbytes):
    return pl.CostEstimate(flops=flops, bytes_accessed=nbytes, transcendentals=0)


def params(mib):
    return pltpu.CompilerParams(vmem_limit_bytes=mib << 20)


def shape(rows, dtype):
    return jax.ShapeDtypeStruct((rows, HALF), dtype)


VMEM = pl.BlockSpec(memory_space=pltpu.VMEM)
HBM = pl.BlockSpec(memory_space=pltpu.HBM)
TILE = 3584
FOLD = HALF // 2


def in_slots(c, o, features):
    slot = lax.broadcasted_iota(jnp.int32, (ROWS, ROWS), 0)
    row = lax.broadcasted_iota(jnp.int32, (ROWS, ROWS), 1)
    a = (slot >> 5) ^ o
    b = (slot >> 3) & 3
    block = jnp.where(c == 0, b * 4 + a, a * 4 + b)
    pick = (block * 8 + (slot & 7) == row).astype(F32).astype(BF16)
    return lax.dot_general(
        pick, features, (((1,), (1,)), ((), ())), preferred_element_type=F32
    ).astype(BF16)


def tiles(source, column, target, sem):
    return [
        pltpu.make_async_copy(
            source.at[:, pl.ds(pl.multiple_of(column + n, 128), TILE)],
            target.at[:, pl.ds(n, TILE)],
            sem.at[n // TILE],
        )
        for n in range(0, HALF, TILE)
    ]


def far_product_kernel(features, grads, out, local, part, value, sem, out_sem):
    c, _, t = place()
    core = 1 - c
    first = pltpu.make_async_copy(features, local, sem.at[HALF // TILE])
    first.start()
    copies = tiles(grads, core * HALF, part, sem)
    for copy in copies:
        copy.start()
    first.wait()
    left = in_slots(core, t, local[...])
    results = tiles(value, 0, out, out_sem)
    for i, (copy, result) in enumerate(zip(copies, results)):
        copy.wait()
        n = slice(i * TILE, (i + 1) * TILE)
        value[:, n] = jnp.dot(left, part[:, n], preferred_element_type=F32).astype(BF16)
        result.start()
    for result in results:
        result.wait()


def far_product(features, grads):
    count = HALF // TILE
    return pl.pallas_call(
        far_product_kernel,
        in_specs=[HBM, HBM],
        out_specs=HBM,
        out_shape=shape(ROWS, BF16),
        scratch_shapes=[
            pltpu.VMEM((TOK, ROWS), BF16),
            pltpu.VMEM((TOK, HALF), BF16),
            pltpu.VMEM((ROWS, HALF), BF16),
            pltpu.SemaphoreType.DMA((count + 1,)),
            pltpu.SemaphoreType.DMA((count,)),
        ],
        cost_estimate=cost(2 * ROWS * TOK * HALF, 4 * TOK * HALF),
        compiler_params=params(60),
    )(features, grads)


def near_product_kernel(features, grads, out, part, sem):
    c, o, _ = place()
    copies = tiles(grads, c * HALF, part, sem)
    for copy in copies:
        copy.start()
    left = in_slots(c, o, features[...])
    for i, copy in enumerate(copies):
        copy.wait()
        n = slice(i * TILE, (i + 1) * TILE)
        out[:, n] = jnp.dot(left, part[:, n], preferred_element_type=F32).astype(BF16)


def near_product(features, grads):
    return pl.pallas_call(
        near_product_kernel,
        in_specs=[VMEM, HBM],
        out_specs=VMEM,
        out_shape=shape(ROWS, BF16),
        scratch_shapes=[pltpu.VMEM((TOK, HALF), BF16), pltpu.SemaphoreType.DMA((HALF // TILE,))],
        cost_estimate=cost(2 * ROWS * TOK * HALF, 4 * TOK * HALF),
        compiler_params=params(12),
    )(features, grads)


def chip_sum_kernel(near, far, own, s1, s2, s3):
    for k, s in ((0, own), (1, s1), (2, s2), (3, s3)):
        n = slice(32 * k, 32 * k + 32)
        s[...] = (near[n, :].astype(F32) + far[n, :].astype(F32)).astype(s.dtype)


def chip_sum(near, far):
    return pl.pallas_call(
        chip_sum_kernel,
        in_specs=[VMEM] * 2,
        out_specs=[VMEM] * 4,
        out_shape=[shape(32, F32)] + [shape(32, BF16)] * 3,
        cost_estimate=cost(ROWS * HALF, 6 * ROWS * HALF),
        compiler_params=params(12),
    )(near, far)


def first_sum_kernel(own, r1, r2, r3, total, out):
    for m in range(0, 32, 4):
        parts = []
        for h in range(2):
            n = (slice(m, m + 4), slice(h * FOLD, (h + 1) * FOLD))
            rest = r1[n].astype(F32) + r2[n].astype(F32) + r3[n].astype(F32)
            parts.append(own[n] + rest)
        value = jnp.concatenate(parts, 0)
        total[2 * m : 2 * m + 8, :] = value
        out[2 * m : 2 * m + 8, :] = value.astype(BF16)


def first_sum(own, parts):
    return pl.pallas_call(
        first_sum_kernel,
        in_specs=[VMEM] * 4,
        out_specs=[VMEM] * 2,
        out_shape=[jax.ShapeDtypeStruct((64, FOLD), d) for d in (F32, BF16)],
        cost_estimate=cost(4 * 32 * HALF, 12 * 32 * HALF),
        compiler_params=params(12),
    )(own, *parts)


def update_kernel(total, parts, mine, theirs, copy, keep, give):
    c, _, t = place()
    own = t * 2 + ((lax.axis_index("fsdp") >> 1) & 1)
    gradient = total[pl.ds(pl.multiple_of(8 * own, 8), 8), :]
    for m in range(8):
        part = parts[8 * m : 8 * m + 8, :].astype(F32)
        gradient += jnp.where(own == m, 0.0, part)

    def folded(i):
        near, far = mine[i].astype(F32), theirs[i].astype(F32)
        low, high = jnp.where(c == 0, near, far), jnp.where(c == 0, far, near)
        rows = [x[:, h * FOLD : (h + 1) * FOLD] for h in range(2) for x in (low, high)]
        return jnp.concatenate(rows, 0)

    initial = folded(0) + noise_scale * folded(1)
    master = adamw(initial, gradient)[0].astype(BF16)
    for m in range(8):
        copy[8 * m : 8 * m + 8, :] = master
    for h in range(2):
        low, high = gradient[4 * h : 4 * h + 2], gradient[4 * h + 2 : 4 * h + 4]
        n = slice(h * FOLD, (h + 1) * FOLD)
        keep[:, n] = jnp.where(c == 0, low, high)
        give[:, n] = jnp.where(c == 0, high, low)


def update(total, parts, mine, theirs):
    return pl.pallas_call(
        update_kernel,
        in_specs=[VMEM] * 4,
        out_specs=[VMEM] * 3,
        out_shape=[jax.ShapeDtypeStruct((64, FOLD), BF16), shape(2, F32), shape(2, F32)],
        cost_estimate=cost(20 * 8 * FOLD, 40 * 8 * FOLD),
        compiler_params=params(12),
    )(total, parts, mine, theirs)


def unfold_kernel(folded, out):
    for t in range(4):
        for h in range(2):
            n = 16 * t + 4 * h
            value = [folded[n + 8 * p : n + 8 * p + 4, :].astype(F32) for p in range(2)]
            out[8 * t : 8 * t + 8, h * FOLD : (h + 1) * FOLD] = jnp.concatenate(value, 0).astype(BF16)


def unfold(folded):
    return pl.pallas_call(
        unfold_kernel,
        in_specs=[VMEM],
        out_specs=VMEM,
        out_shape=shape(32, BF16),
        cost_estimate=cost(0, 4 * 32 * HALF),
        compiler_params=params(12),
    )(folded)


def assemble_kernel(pieces, *refs):
    c, o, t = place()
    blocks, out, sem = refs[: len(pieces)], refs[-2], refs[-1]
    copies = []
    for block, (half, k) in zip(blocks, pieces):
        core, a = (c, o ^ k) if half == 0 else (1 - c, t ^ k)
        for j in range(4):
            row = jnp.where(core == 0, j * 4 + a, a * 4 + j) * 8
            copies.append(
                pltpu.make_async_copy(
                    block.at[pl.ds(8 * j, 8)],
                    out.at[
                        pl.ds(pl.multiple_of(row, 8), 8),
                        pl.ds(pl.multiple_of(core * HALF, 128), HALF),
                    ],
                    sem.at[len(copies)],
                )
            )
    for copy in copies:
        copy.start()
    for copy in copies:
        copy.wait()


def assemble(pieces, blocks, result=None):
    operands = list(blocks) if result is None else list(blocks) + [result]
    return pl.pallas_call(
        functools.partial(assemble_kernel, pieces),
        in_specs=[pl.BlockSpec(memory_space=pl.ANY)] * len(blocks)
        + [HBM] * (len(operands) - len(blocks)),
        out_specs=HBM,
        out_shape=jax.ShapeDtypeStruct((ROWS, FF), BF16),
        scratch_shapes=[pltpu.SemaphoreType.DMA((4 * len(pieces),))],
        input_output_aliases={} if result is None else {len(blocks): 0},
        cost_estimate=cost(0, len(pieces) * ROWS * HALF),
        compiler_params=params(12),
    )(*operands)


def in_order(bit, mine, theirs, axis):
    lower = jnp.where(bit == 0, mine, theirs)
    upper = jnp.where(bit == 0, theirs, mine)
    return jnp.concatenate([lower, upper], axis)


def body(dense_rows, noise, features, out_grads):
    c = lax.axis_index("fsdp") & 1

    grads = out_grads[0]
    far = send(far_product(features[0], grads), other_core)
    near = near_product(features[0], grads)
    own, *chunks = chip_sum(near, far)
    got = [send(chunks[k - 1], wide(k)) for k in (2, 1, 3)]
    total, rounded = first_sum(own, got)

    dense = lax.all_to_all(jnp.stack([dense_rows] * 8), "expert", 0, 0, tiled=True)
    dense = dense.swapaxes(0, 1).reshape(2, FF)
    both = jnp.stack([dense, noise[0]])
    mine = lax.dynamic_slice(both, (0, 0, c * HALF), (2, 2, HALF))
    theirs = send(lax.dynamic_slice(both, (0, 0, (1 - c) * HALF), (2, 2, HALF)), other_core)

    copy, keep, give = update(total, swap(rounded), mine, theirs)
    own = unfold(swap(copy))
    r1, r3, r2 = (send(own, wide(k)) for k in (1, 3, 2))
    x0, x1, x3, x2 = (send(x, other_core) for x in (own, r1, r3, r2))
    early = assemble(((0, 0), (0, 1), (1, 0), (1, 1)), (own, r1, x0, x1))
    expert_copy = assemble(((0, 2), (0, 3), (1, 2), (1, 3)), (r2, r3, x2, x3), early)
    give, _ = lax.optimization_barrier((give, r1))

    gradient = in_order(c, keep, send(give, other_core), 1)
    initial = dense.astype(F32) + noise_scale * noise[0].astype(F32)
    master, first_moment, second_moment = adamw(initial, gradient)
    return (master[None], first_moment[None], second_moment[None], expert_copy[None])


def solution(mesh):
    return jax.shard_map(
        body,
        mesh=mesh,
        in_specs=(
            P("fsdp", "expert"),
            P("expert", "fsdp", None),
            P("expert", "fsdp", None),
            P("expert", "fsdp", None),
        ),
        out_specs=(
            P("expert", "fsdp", None),
            P("expert", "fsdp", None),
            P("expert", "fsdp", None),
            P("expert", None, None),
        ),
        check_vma=False,
    )
```

```python
import functools

import jax
import jax.numpy as jnp
from jax import lax
from jax.experimental import pallas as pl
from jax.experimental.pallas import tpu as pltpu
from jax.sharding import PartitionSpec as P

noise_scale = 0.1
first_decay = 0.9
second_decay = 0.95
learn_rate = 0.2
weight_decay = 0.5
epsilon_adam = 1.0

FF = 14336
HALF = FF // 2
ROWS = 128
TOK = 128
NZ, NY = 4, 8
F32 = jnp.float32
BF16 = jnp.bfloat16


def index(z, y, c):
    return (z * NY + y) * 2 + c


def perm(target):
    return [
        (index(z, y, c), index(*target(z, y, c)))
        for z in range(NZ)
        for y in range(NY)
        for c in range(2)
    ]


def send(x, target):
    return lax.ppermute(x, "fsdp", perm(target))


def along_y(z, y, c, k):
    return (z, 2 * ((y // 2) ^ k) + y % 2, c)


def along_z(z, y, c, k):
    return (z ^ k, y, c)


def wide(k):
    return lambda z, y, c: along_y(z, y, c, k) if c == 0 else along_z(z, y, c, k)


MIDDLE = [[index(z, 2 * q + p, 0) for z in range(NZ) for p in range(2)] for q in range(4)] + [
    [index(z, y, 1) for y in range(NY)] for z in range(NZ)
]


def swap(x):
    return lax.all_to_all(x, "fsdp", 0, 0, axis_index_groups=MIDDLE, tiled=True)


def other_core(z, y, c):
    return (z, y, 1 - c)


def adamw(initial, gradient):
    first_moment = (1.0 - first_decay) * gradient
    second_moment = (1.0 - second_decay) * gradient * gradient
    update = (
        first_moment
        / (1.0 - first_decay)
        / (jnp.sqrt(second_moment / (1.0 - second_decay)) + epsilon_adam)
    )
    master = initial - learn_rate * (update + weight_decay * initial)
    return (master, first_moment, second_moment)


def place():
    f = lax.axis_index("fsdp")
    c, q, z = f & 1, (f >> 2) & 3, f >> 4
    return c, jnp.where(c == 0, q, z), jnp.where(c == 0, z, q)


def cost(flops, nbytes):
    return pl.CostEstimate(flops=flops, bytes_accessed=nbytes, transcendentals=0)


def params(mib):
    return pltpu.CompilerParams(vmem_limit_bytes=mib << 20)


def shape(rows, dtype):
    return jax.ShapeDtypeStruct((rows, HALF), dtype)


VMEM = pl.BlockSpec(memory_space=pltpu.VMEM)
HBM = pl.BlockSpec(memory_space=pltpu.HBM)
TILE = 3584
FOLD = HALF // 2


def in_slots(c, o, features):
    slot = lax.broadcasted_iota(jnp.int32, (ROWS, ROWS), 0)
    row = lax.broadcasted_iota(jnp.int32, (ROWS, ROWS), 1)
    a = (slot >> 5) ^ o
    b = (slot >> 3) & 3
    block = jnp.where(c == 0, b * 4 + a, a * 4 + b)
    pick = (block * 8 + (slot & 7) == row).astype(F32).astype(BF16)
    return lax.dot_general(
        pick, features, (((1,), (1,)), ((), ())), preferred_element_type=F32
    ).astype(BF16)


def tiles(source, column, target, sem):
    return [
        pltpu.make_async_copy(
            source.at[:, pl.ds(pl.multiple_of(column + n, 128), TILE)],
            target.at[:, pl.ds(n, TILE)],
            sem.at[n // TILE],
        )
        for n in range(0, HALF, TILE)
    ]


def far_product_kernel(features, grads, out, local, part, value, sem, out_sem):
    c, _, t = place()
    core = 1 - c
    first = pltpu.make_async_copy(features, local, sem.at[HALF // TILE])
    first.start()
    copies = tiles(grads, core * HALF, part, sem)
    for copy in copies:
        copy.start()
    first.wait()
    left = in_slots(core, t, local[...])
    results = tiles(value, 0, out, out_sem)
    for i, (copy, result) in enumerate(zip(copies, results)):
        copy.wait()
        n = slice(i * TILE, (i + 1) * TILE)
        value[:, n] = jnp.dot(left, part[:, n], preferred_element_type=F32).astype(BF16)
        result.start()
    for result in results:
        result.wait()


def far_product(features, grads):
    count = HALF // TILE
    return pl.pallas_call(
        far_product_kernel,
        in_specs=[HBM, HBM],
        out_specs=HBM,
        out_shape=shape(ROWS, BF16),
        scratch_shapes=[
            pltpu.VMEM((TOK, ROWS), BF16),
            pltpu.VMEM((TOK, HALF), BF16),
            pltpu.VMEM((ROWS, HALF), BF16),
            pltpu.SemaphoreType.DMA((count + 1,)),
            pltpu.SemaphoreType.DMA((count,)),
        ],
        cost_estimate=cost(2 * ROWS * TOK * HALF, 4 * TOK * HALF),
        compiler_params=params(60),
    )(features, grads)


def near_product_kernel(features, grads, out, part, sem):
    c, o, _ = place()
    copies = tiles(grads, c * HALF, part, sem)
    for copy in copies:
        copy.start()
    left = in_slots(c, o, features[...])
    for i, copy in enumerate(copies):
        copy.wait()
        n = slice(i * TILE, (i + 1) * TILE)
        out[:, n] = jnp.dot(left, part[:, n], preferred_element_type=F32).astype(BF16)


def near_product(features, grads):
    return pl.pallas_call(
        near_product_kernel,
        in_specs=[VMEM, HBM],
        out_specs=VMEM,
        out_shape=shape(ROWS, BF16),
        scratch_shapes=[pltpu.VMEM((TOK, HALF), BF16), pltpu.SemaphoreType.DMA((HALF // TILE,))],
        cost_estimate=cost(2 * ROWS * TOK * HALF, 4 * TOK * HALF),
        compiler_params=params(12),
    )(features, grads)


def chip_sum_kernel(near, far, own, s1, s2, s3):
    for k, s in ((0, own), (1, s1), (2, s2), (3, s3)):
        n = slice(32 * k, 32 * k + 32)
        s[...] = (near[n, :].astype(F32) + far[n, :].astype(F32)).astype(s.dtype)


def chip_sum(near, far):
    return pl.pallas_call(
        chip_sum_kernel,
        in_specs=[VMEM] * 2,
        out_specs=[VMEM] * 4,
        out_shape=[shape(32, F32)] + [shape(32, BF16)] * 3,
        cost_estimate=cost(ROWS * HALF, 6 * ROWS * HALF),
        compiler_params=params(12),
    )(near, far)


def first_sum_kernel(own, r1, r2, r3, total, out):
    for m in range(0, 32, 8):
        n = slice(m, m + 8)
        value = own[n, :] + (r1[n, :].astype(F32) + r2[n, :].astype(F32) + r3[n, :].astype(F32))
        for i in range(2):
            rows = value[4 * i : 4 * i + 4]
            folded = jnp.concatenate([rows[:, :FOLD], rows[:, FOLD:]], 0)
            start = 2 * m + 8 * i
            total[start : start + 8, :] = folded
            out[start : start + 8, :] = folded.astype(BF16)


def first_sum(own, parts):
    return pl.pallas_call(
        first_sum_kernel,
        in_specs=[VMEM] * 4,
        out_specs=[VMEM] * 2,
        out_shape=[jax.ShapeDtypeStruct((64, FOLD), d) for d in (F32, BF16)],
        cost_estimate=cost(4 * 32 * HALF, 12 * 32 * HALF),
        compiler_params=params(12),
    )(own, *parts)


def update_kernel(total, parts, mine, theirs, copy, keep, give):
    c, _, t = place()
    own = t * 2 + ((lax.axis_index("fsdp") >> 1) & 1)
    gradient = total[pl.ds(pl.multiple_of(8 * own, 8), 8), :]
    for m in range(8):
        part = parts[8 * m : 8 * m + 8, :].astype(F32)
        gradient += jnp.where(own == m, 0.0, part)

    def folded(i):
        near, far = mine[i].astype(F32), theirs[i].astype(F32)
        low, high = jnp.where(c == 0, near, far), jnp.where(c == 0, far, near)
        rows = [x[:, h * FOLD : (h + 1) * FOLD] for h in range(2) for x in (low, high)]
        return jnp.concatenate(rows, 0)

    initial = folded(0) + noise_scale * folded(1)
    master = adamw(initial, gradient)[0].astype(BF16)
    for m in range(8):
        copy[8 * m : 8 * m + 8, :] = master
    for h in range(2):
        low, high = gradient[4 * h : 4 * h + 2], gradient[4 * h + 2 : 4 * h + 4]
        n = slice(h * FOLD, (h + 1) * FOLD)
        keep[:, n] = jnp.where(c == 0, low, high)
        give[:, n] = jnp.where(c == 0, high, low)


def update(total, parts, mine, theirs):
    return pl.pallas_call(
        update_kernel,
        in_specs=[VMEM] * 4,
        out_specs=[VMEM] * 3,
        out_shape=[jax.ShapeDtypeStruct((64, FOLD), BF16), shape(2, F32), shape(2, F32)],
        cost_estimate=cost(20 * 8 * FOLD, 40 * 8 * FOLD),
        compiler_params=params(12),
    )(total, parts, mine, theirs)


def unfold_kernel(folded, out):
    for t in range(4):
        for h in range(2):
            n = 16 * t + 4 * h
            value = [folded[n + 8 * p : n + 8 * p + 4, :].astype(F32) for p in range(2)]
            out[8 * t : 8 * t + 8, h * FOLD : (h + 1) * FOLD] = jnp.concatenate(value, 0).astype(BF16)


def unfold(folded):
    return pl.pallas_call(
        unfold_kernel,
        in_specs=[VMEM],
        out_specs=VMEM,
        out_shape=shape(32, BF16),
        cost_estimate=cost(0, 4 * 32 * HALF),
        compiler_params=params(12),
    )(folded)


def assemble_kernel(pieces, *refs):
    c, o, t = place()
    blocks, out, sem = refs[: len(pieces)], refs[-2], refs[-1]
    copies = []
    for block, (half, k) in zip(blocks, pieces):
        core, a = (c, o ^ k) if half == 0 else (1 - c, t ^ k)
        for j in range(4):
            row = jnp.where(core == 0, j * 4 + a, a * 4 + j) * 8
            copies.append(
                pltpu.make_async_copy(
                    block.at[pl.ds(8 * j, 8)],
                    out.at[
                        pl.ds(pl.multiple_of(row, 8), 8),
                        pl.ds(pl.multiple_of(core * HALF, 128), HALF),
                    ],
                    sem.at[len(copies)],
                )
            )
    for copy in copies:
        copy.start()
    for copy in copies:
        copy.wait()


def assemble(pieces, blocks, result=None):
    operands = list(blocks) if result is None else list(blocks) + [result]
    return pl.pallas_call(
        functools.partial(assemble_kernel, pieces),
        in_specs=[pl.BlockSpec(memory_space=pl.ANY)] * len(blocks)
        + [HBM] * (len(operands) - len(blocks)),
        out_specs=HBM,
        out_shape=jax.ShapeDtypeStruct((ROWS, FF), BF16),
        scratch_shapes=[pltpu.SemaphoreType.DMA((4 * len(pieces),))],
        input_output_aliases={} if result is None else {len(blocks): 0},
        cost_estimate=cost(0, len(pieces) * ROWS * HALF),
        compiler_params=params(12),
    )(*operands)


def in_order(bit, mine, theirs, axis):
    lower = jnp.where(bit == 0, mine, theirs)
    upper = jnp.where(bit == 0, theirs, mine)
    return jnp.concatenate([lower, upper], axis)


def body(dense_rows, noise, features, out_grads):
    c = lax.axis_index("fsdp") & 1

    grads = out_grads[0]
    far = send(far_product(features[0], grads), other_core)
    near = near_product(features[0], grads)
    own, *chunks = chip_sum(near, far)
    got = [send(chunks[k - 1], wide(k)) for k in (2, 1, 3)]
    total, rounded = first_sum(own, got)

    dense = lax.all_to_all(jnp.stack([dense_rows] * 8), "expert", 0, 0, tiled=True)
    dense = dense.swapaxes(0, 1).reshape(2, FF)
    both = jnp.stack([dense, noise[0]])
    mine = lax.dynamic_slice(both, (0, 0, c * HALF), (2, 2, HALF))
    theirs = send(lax.dynamic_slice(both, (0, 0, (1 - c) * HALF), (2, 2, HALF)), other_core)

    copy, keep, give = update(total, swap(rounded), mine, theirs)
    own = unfold(swap(copy))
    r1, r3, r2 = (send(own, wide(k)) for k in (1, 3, 2))
    x0, x1, x3, x2 = (send(x, other_core) for x in (own, r1, r3, r2))
    early = assemble(((0, 0), (0, 1), (1, 0), (1, 1)), (own, r1, x0, x1))
    expert_copy = assemble(((0, 2), (0, 3), (1, 2), (1, 3)), (r2, r3, x2, x3), early)
    give, _ = lax.optimization_barrier((give, r1))

    gradient = in_order(c, keep, send(give, other_core), 1)
    initial = dense.astype(F32) + noise_scale * noise[0].astype(F32)
    master, first_moment, second_moment = adamw(initial, gradient)
    return (master[None], first_moment[None], second_moment[None], expert_copy[None])


def solution(mesh):
    return jax.shard_map(
        body,
        mesh=mesh,
        in_specs=(
            P("fsdp", "expert"),
            P("expert", "fsdp", None),
            P("expert", "fsdp", None),
            P("expert", "fsdp", None),
        ),
        out_specs=(
            P("expert", "fsdp", None),
            P("expert", "fsdp", None),
            P("expert", "fsdp", None),
            P("expert", None, None),
        ),
        check_vma=False,
    )
```

```python
import functools

import jax
import jax.numpy as jnp
from jax import lax
from jax.experimental import pallas as pl
from jax.experimental.pallas import tpu as pltpu
from jax.sharding import PartitionSpec as P

noise_scale = 0.1
first_decay = 0.9
second_decay = 0.95
learn_rate = 0.2
weight_decay = 0.5
epsilon_adam = 1.0

FF = 14336
HALF = FF // 2
ROWS = 128
TOK = 128
NZ, NY = 4, 8
F32 = jnp.float32
BF16 = jnp.bfloat16


def index(z, y, c):
    return (z * NY + y) * 2 + c


def perm(target):
    return [
        (index(z, y, c), index(*target(z, y, c)))
        for z in range(NZ)
        for y in range(NY)
        for c in range(2)
    ]


def send(x, target):
    return lax.ppermute(x, "fsdp", perm(target))


def along_y(z, y, c, k):
    return (z, 2 * ((y // 2) ^ k) + y % 2, c)


def along_z(z, y, c, k):
    return (z ^ k, y, c)


def wide(k):
    return lambda z, y, c: along_y(z, y, c, k) if c == 0 else along_z(z, y, c, k)


MIDDLE = [[index(z, 2 * q + p, 0) for z in range(NZ) for p in range(2)] for q in range(4)] + [
    [index(z, y, 1) for y in range(NY)] for z in range(NZ)
]


def swap(x):
    return lax.all_to_all(x, "fsdp", 0, 0, axis_index_groups=MIDDLE, tiled=True)


def other_core(z, y, c):
    return (z, y, 1 - c)


def adamw(initial, gradient):
    first_moment = (1.0 - first_decay) * gradient
    second_moment = (1.0 - second_decay) * gradient * gradient
    update = (
        first_moment
        / (1.0 - first_decay)
        / (jnp.sqrt(second_moment / (1.0 - second_decay)) + epsilon_adam)
    )
    master = initial - learn_rate * (update + weight_decay * initial)
    return (master, first_moment, second_moment)


def place():
    f = lax.axis_index("fsdp")
    c, q, z = f & 1, (f >> 2) & 3, f >> 4
    return c, jnp.where(c == 0, q, z), jnp.where(c == 0, z, q)


def cost(flops, nbytes):
    return pl.CostEstimate(flops=flops, bytes_accessed=nbytes, transcendentals=0)


def params(mib):
    return pltpu.CompilerParams(vmem_limit_bytes=mib << 20)


def shape(rows, dtype):
    return jax.ShapeDtypeStruct((rows, HALF), dtype)


VMEM = pl.BlockSpec(memory_space=pltpu.VMEM)
HBM = pl.BlockSpec(memory_space=pltpu.HBM)
TILE = 3584
FOLD = HALF // 2


def in_slots(c, o, features):
    slot = lax.broadcasted_iota(jnp.int32, (ROWS, ROWS), 0)
    row = lax.broadcasted_iota(jnp.int32, (ROWS, ROWS), 1)
    a = (slot >> 5) ^ o
    b = (slot >> 3) & 3
    block = jnp.where(c == 0, b * 4 + a, a * 4 + b)
    pick = (block * 8 + (slot & 7) == row).astype(F32).astype(BF16)
    return lax.dot_general(
        pick, features, (((1,), (1,)), ((), ())), preferred_element_type=F32
    ).astype(BF16)


def tiles(source, column, target, sem):
    return [
        pltpu.make_async_copy(
            source.at[:, pl.ds(pl.multiple_of(column + n, 128), TILE)],
            target.at[:, pl.ds(n, TILE)],
            sem.at[n // TILE],
        )
        for n in range(0, HALF, TILE)
    ]


def far_product_kernel(features, grads, out, local, part, value, sem, out_sem):
    c, _, t = place()
    core = 1 - c
    first = pltpu.make_async_copy(features, local, sem.at[HALF // TILE])
    first.start()
    copies = tiles(grads, core * HALF, part, sem)
    for copy in copies:
        copy.start()
    first.wait()
    left = in_slots(core, t, local[...])
    results = tiles(value, 0, out, out_sem)
    for i, (copy, result) in enumerate(zip(copies, results)):
        copy.wait()
        n = slice(i * TILE, (i + 1) * TILE)
        value[:, n] = jnp.dot(left, part[:, n], preferred_element_type=F32).astype(BF16)
        result.start()
    for result in results:
        result.wait()


def far_product(features, grads):
    count = HALF // TILE
    return pl.pallas_call(
        far_product_kernel,
        in_specs=[HBM, HBM],
        out_specs=HBM,
        out_shape=shape(ROWS, BF16),
        scratch_shapes=[
            pltpu.VMEM((TOK, ROWS), BF16),
            pltpu.VMEM((TOK, HALF), BF16),
            pltpu.VMEM((ROWS, HALF), BF16),
            pltpu.SemaphoreType.DMA((count + 1,)),
            pltpu.SemaphoreType.DMA((count,)),
        ],
        cost_estimate=cost(2 * ROWS * TOK * HALF, 4 * TOK * HALF),
        compiler_params=params(60),
    )(features, grads)


def near_product_kernel(features, grads, out, part, sem):
    c, o, _ = place()
    copies = tiles(grads, c * HALF, part, sem)
    for copy in copies:
        copy.start()
    left = in_slots(c, o, features[...])
    for i, copy in enumerate(copies):
        copy.wait()
        n = slice(i * TILE, (i + 1) * TILE)
        out[:, n] = jnp.dot(left, part[:, n], preferred_element_type=F32).astype(BF16)


def near_product(features, grads):
    return pl.pallas_call(
        near_product_kernel,
        in_specs=[VMEM, HBM],
        out_specs=VMEM,
        out_shape=shape(ROWS, BF16),
        scratch_shapes=[pltpu.VMEM((TOK, HALF), BF16), pltpu.SemaphoreType.DMA((HALF // TILE,))],
        cost_estimate=cost(2 * ROWS * TOK * HALF, 4 * TOK * HALF),
        compiler_params=params(12),
    )(features, grads)


def chip_sum_kernel(near, far, own, s1, s2, s3):
    for k, s in ((0, own), (1, s1), (2, s2), (3, s3)):
        n = slice(32 * k, 32 * k + 32)
        s[...] = (near[n, :].astype(F32) + far[n, :].astype(F32)).astype(s.dtype)


def chip_sum(near, far):
    return pl.pallas_call(
        chip_sum_kernel,
        in_specs=[VMEM] * 2,
        out_specs=[VMEM] * 4,
        out_shape=[shape(32, F32)] + [shape(32, BF16)] * 3,
        cost_estimate=cost(ROWS * HALF, 6 * ROWS * HALF),
        compiler_params=params(12),
    )(near, far)


def first_sum_kernel(own, r1, r2, r3, total, out):
    for m in range(0, 32, 4):
        parts = []
        for h in range(2):
            n = (slice(m, m + 4), slice(h * FOLD, (h + 1) * FOLD))
            rest = r1[n].astype(F32) + r2[n].astype(F32) + r3[n].astype(F32)
            parts.append(own[n] + rest)
        value = jnp.concatenate(parts, 0)
        total[2 * m : 2 * m + 8, :] = value
        out[2 * m : 2 * m + 8, :] = value.astype(BF16)


def first_sum(own, parts):
    return pl.pallas_call(
        first_sum_kernel,
        in_specs=[VMEM] * 4,
        out_specs=[VMEM] * 2,
        out_shape=[jax.ShapeDtypeStruct((64, FOLD), d) for d in (F32, BF16)],
        cost_estimate=cost(4 * 32 * HALF, 12 * 32 * HALF),
        compiler_params=params(12),
    )(own, *parts)


def update_kernel(total, parts, mine, theirs, copy, keep, give):
    c, _, t = place()
    own = t * 2 + ((lax.axis_index("fsdp") >> 1) & 1)
    gradient = total[pl.ds(pl.multiple_of(8 * own, 8), 8), :]
    for m in range(8):
        part = parts[8 * m : 8 * m + 8, :].astype(F32)
        gradient += jnp.where(own == m, 0.0, part)

    def folded(i):
        near, far = mine[i].astype(F32), theirs[i].astype(F32)
        low, high = jnp.where(c == 0, near, far), jnp.where(c == 0, far, near)
        rows = [x[:, h * FOLD : (h + 1) * FOLD] for h in range(2) for x in (low, high)]
        return jnp.concatenate(rows, 0)

    initial = folded(0) + noise_scale * folded(1)
    master = adamw(initial, gradient)[0].astype(BF16)
    for m in range(8):
        copy[8 * m : 8 * m + 8, :] = master
    for h in range(2):
        low, high = gradient[4 * h : 4 * h + 2], gradient[4 * h + 2 : 4 * h + 4]
        n = slice(h * FOLD, (h + 1) * FOLD)
        keep[:, n] = jnp.where(c == 0, low, high)
        give[:, n] = jnp.where(c == 0, high, low)


def update(total, parts, mine, theirs):
    return pl.pallas_call(
        update_kernel,
        in_specs=[VMEM] * 4,
        out_specs=[VMEM] * 3,
        out_shape=[jax.ShapeDtypeStruct((64, FOLD), BF16), shape(2, F32), shape(2, F32)],
        cost_estimate=cost(20 * 8 * FOLD, 40 * 8 * FOLD),
        compiler_params=params(12),
    )(total, parts, mine, theirs)


def unfold_kernel(folded, out):
    for t in range(4):
        for h in range(2):
            n = 16 * t + 4 * h
            value = [folded[n + 8 * p : n + 8 * p + 4, :].astype(F32) for p in range(2)]
            out[8 * t : 8 * t + 8, h * FOLD : (h + 1) * FOLD] = jnp.concatenate(value, 0).astype(BF16)


def unfold(folded):
    return pl.pallas_call(
        unfold_kernel,
        in_specs=[VMEM],
        out_specs=VMEM,
        out_shape=shape(32, BF16),
        cost_estimate=cost(0, 4 * 32 * HALF),
        compiler_params=params(12),
    )(folded)


def assemble_kernel(pieces, *refs):
    c, o, t = place()
    blocks, out, sem = refs[: len(pieces)], refs[-2], refs[-1]
    copies = []
    for block, (half, k) in zip(blocks, pieces):
        core, a = (c, o ^ k) if half == 0 else (1 - c, t ^ k)
        for j in range(4):
            row = jnp.where(core == 0, j * 4 + a, a * 4 + j) * 8
            copies.append(
                pltpu.make_async_copy(
                    block.at[pl.ds(8 * j, 8)],
                    out.at[
                        pl.ds(pl.multiple_of(row, 8), 8),
                        pl.ds(pl.multiple_of(core * HALF, 128), HALF),
                    ],
                    sem.at[len(copies)],
                )
            )
    for copy in copies:
        copy.start()
    for copy in copies:
        copy.wait()


def assemble(pieces, blocks, result=None):
    operands = list(blocks) if result is None else list(blocks) + [result]
    return pl.pallas_call(
        functools.partial(assemble_kernel, pieces),
        in_specs=[pl.BlockSpec(memory_space=pl.ANY)] * len(blocks)
        + [HBM] * (len(operands) - len(blocks)),
        out_specs=HBM,
        out_shape=jax.ShapeDtypeStruct((ROWS, FF), BF16),
        scratch_shapes=[pltpu.SemaphoreType.DMA((4 * len(pieces),))],
        input_output_aliases={} if result is None else {len(blocks): 0},
        cost_estimate=cost(0, len(pieces) * ROWS * HALF),
        compiler_params=params(12),
    )(*operands)


def in_order(bit, mine, theirs, axis):
    lower = jnp.where(bit == 0, mine, theirs)
    upper = jnp.where(bit == 0, theirs, mine)
    return jnp.concatenate([lower, upper], axis)


def body(dense_rows, noise, features, out_grads):
    c = lax.axis_index("fsdp") & 1

    grads = out_grads[0]
    far = send(far_product(features[0], grads), other_core)
    near = near_product(features[0], grads)
    own, *chunks = chip_sum(near, far)
    got = [send(chunks[k - 1], wide(k)) for k in (1, 3, 2)]
    total, rounded = first_sum(own, got)

    dense = lax.all_to_all(jnp.stack([dense_rows] * 8), "expert", 0, 0, tiled=True)
    dense = dense.swapaxes(0, 1).reshape(2, FF)
    both = jnp.stack([dense, noise[0]])
    mine = lax.dynamic_slice(both, (0, 0, c * HALF), (2, 2, HALF))
    theirs = send(lax.dynamic_slice(both, (0, 0, (1 - c) * HALF), (2, 2, HALF)), other_core)

    copy, keep, give = update(total, swap(rounded), mine, theirs)
    own = unfold(swap(copy))
    r1, r3, r2 = (send(own, wide(k)) for k in (1, 3, 2))
    x0, x1, x3, x2 = (send(x, other_core) for x in (own, r1, r3, r2))
    early = assemble(((0, 0), (0, 1), (1, 0), (1, 1)), (own, r1, x0, x1))
    expert_copy = assemble(((0, 2), (0, 3), (1, 2), (1, 3)), (r2, r3, x2, x3), early)
    give, _ = lax.optimization_barrier((give, r1))

    gradient = in_order(c, keep, send(give, other_core), 1)
    initial = dense.astype(F32) + noise_scale * noise[0].astype(F32)
    master, first_moment, second_moment = adamw(initial, gradient)
    return (master[None], first_moment[None], second_moment[None], expert_copy[None])


def solution(mesh):
    return jax.shard_map(
        body,
        mesh=mesh,
        in_specs=(
            P("fsdp", "expert"),
            P("expert", "fsdp", None),
            P("expert", "fsdp", None),
            P("expert", "fsdp", None),
        ),
        out_specs=(
            P("expert", "fsdp", None),
            P("expert", "fsdp", None),
            P("expert", "fsdp", None),
            P("expert", None, None),
        ),
        check_vma=False,
    )
```
